32 devices in a mesh: blk: 8 (over z, y), ch: 4 (over x, core).
Axes of the slice: x: 2, y: 2, z: 4, core: 2. Of those that a mesh axis runs over, the one named last changes fastest.
Arguments:
- features: bfloat16 [6144, 512], P('blk', 'ch'), may hold values from -6 to 6
- tile_values: bfloat16 [1024, 128, 128], P('blk'), may hold values from -600 to 600
- tile_source: int32 [1024], P('blk'), may hold values from 0 to 48, as said below
- tile_target: int32 [1024], P('blk'), may hold values from 0 to 5
- tile_count: int32 [8], P('blk'), may hold values from 32 to 128
- weights: bfloat16 [3, 512, 512], replicated, may hold values from -0.15625 to 0.15625
- bias_vector: float32 [512], replicated, may hold values from -3 to 3
Outputs:
- mixed: bfloat16 [6144, 512], P('blk', 'ch')
The draws below stay inside these ranges and needn't reach their ends.
Inputs may be any that keep to these rules, and one draw needn't show every extreme that they name: `tile_source`: in each index of blk the live slots come first, sorted by value, and at most 32 of them name row tiles of one index of blk (tiles 6 * b to 6 * b + 5), a bound that every index of blk reaches; slots from tile_count on hold 48.
All inputs are finite; a program needn't handle non-finite values.
Results may differ from the reference program's by a relative error of at most 0.01.
Values may be sent and summed in bfloat16 or wider, within the bound.
A program may use at most 64 MiB of HBM per device.

```python
import math
import jax
import jax.numpy as jnp
from jax import lax

CHANNELS = 512
TILE = 128
RT_DEV = 6
TILES_DEV = 128
ROWS_DEV = 768
SCAP = 32
GATES = 6144
N_BLK = 8


def pattern(key):
    base_key = jax.random.fold_in(key, 11)
    full_dev = jax.random.randint(jax.random.fold_in(base_key, 1), (), 0, N_BLK)
    low_dev = (full_dev + 1 + jax.random.randint(jax.random.fold_in(base_key, 2), (), 0, N_BLK - 1)) % N_BLK

    def per_device(device):
        device_key = jax.random.fold_in(base_key, 100 + device)
        shuffled = jax.random.permutation(jax.random.fold_in(device_key, 1), (N_BLK - 1) * SCAP).astype(jnp.int32)
        lead_block = jax.random.randint(jax.random.fold_in(device_key, 2), (), 0, N_BLK).astype(jnp.int32)
        others = shuffled[:TILES_DEV - SCAP] // SCAP
        others = others + (others >= lead_block).astype(jnp.int32)
        blocks = jnp.concatenate([jnp.full((SCAP,), lead_block, jnp.int32), others])
        within = jax.random.randint(jax.random.fold_in(device_key, 3), (TILES_DEV,), 0, RT_DEV).astype(jnp.int32)
        halving = jax.random.randint(jax.random.fold_in(device_key, 4), (), 0, 2).astype(jnp.int32)
        live_count = jnp.right_shift(jnp.int32(TILES_DEV), halving)
        live_count = jnp.where(device == full_dev, TILES_DEV, jnp.where(device == low_dev, TILES_DEV // 4, live_count)).astype(jnp.int32)
        usable = jnp.arange(TILES_DEV, dtype=jnp.int32) < live_count
        sort_keys = jnp.where(usable, blocks * RT_DEV + within, N_BLK * RT_DEV).astype(jnp.int32)
        return (jnp.sort(sort_keys), live_count)
    sources, counts = jax.vmap(per_device)(jnp.arange(N_BLK, dtype=jnp.int32))
    return (sources.reshape(-1).astype(jnp.int32), counts.astype(jnp.int32))


def draw_tile_source(key, part):
    return pattern(key)[0]


def draw_tile_count(key, part):
    return pattern(key)[1]


def draw_tile_values(key, part):
    shape = (N_BLK * TILES_DEV, TILE, TILE)
    base_part = jnp.clip(jax.random.normal(jax.random.fold_in(key, 1), shape, jnp.float32), -6.0, 6.0)
    log_top = math.log(10.0)
    row_scale = jnp.exp(jax.random.uniform(jax.random.fold_in(key, 2), (N_BLK * TILES_DEV, TILE, 1), jnp.float32, 0.0, log_top))
    col_scale = jnp.exp(jax.random.uniform(jax.random.fold_in(key, 3), (N_BLK * TILES_DEV, 1, TILE), jnp.float32, 0.0, log_top))
    return jnp.clip(base_part * row_scale * col_scale, -600.0, 600.0).astype(jnp.bfloat16)


def place_ends(array, key, least, largest):
    longest = array.shape.index(max(array.shape))
    spots = []
    for shift in (0, 1):
        where = [jax.random.randint(jax.random.fold_in(key, axis), (), 0, length) for axis, length in enumerate(array.shape)]
        where[longest] = (where[longest] + shift) % array.shape[longest]
        spots.append(tuple(where))
    return array.at[spots[0]].set(least).at[spots[1]].set(largest)


def levels(own_key, extent, pieces, smallest, top_value):
    gain = 1.0
    for axis_at, blocks in pieces:
        draws = jax.random.uniform(jax.random.fold_in(jax.random.fold_in(own_key, 6), axis_at), (blocks,), jnp.float32, smallest / len(pieces), top_value / len(pieces))
        gain = gain * jnp.repeat(jnp.exp(draws), extent[axis_at] // blocks).reshape((-1,) + (1,) * (len(extent) - 1 - axis_at))
    return gain


def scatter_about(key, extent, scale, limit, shards=(), kind=jnp.bfloat16):
    entries = jax.random.normal(key, extent, jnp.float32) * scale
    if len(shards) > 0:
        entries = levels(key, extent, shards, -0.22, 0.18) * entries
    return jnp.clip(entries, min=-limit, max=limit).astype(kind)


def setup_inputs(seed: int = 0) -> dict:
    keys = jax.random.split(jax.random.key(seed), 8)
    return {
        "features": scatter_about(keys[0], (GATES, CHANNELS), 1.0, 6.0, ((0, 8), (1, 4))),
        "tile_values": draw_tile_values(jax.random.fold_in(keys[7], 71), 0),
        "tile_source": draw_tile_source(jax.random.fold_in(keys[7], 71), 0),
        "tile_target": place_ends(jax.random.randint(keys[3], (N_BLK * TILES_DEV,), 0, RT_DEV), jax.random.fold_in(keys[3], 1), 0, RT_DEV - 1).astype(jnp.int32),
        "tile_count": draw_tile_count(jax.random.fold_in(keys[7], 71), 0),
        "weights": scatter_about(keys[5], (3, CHANNELS, CHANNELS), (3 * CHANNELS) ** -0.5, 0.15625),
        "bias_vector": scatter_about(keys[6], (CHANNELS,), 0.5, 3.0, (), jnp.float32),
    }


def propagate(signal, tile_values, tile_source, tile_target, tile_count):
    blocks = signal.reshape(N_BLK * RT_DEV, TILE, CHANNELS)

    def per_device(device):
        first_tile = (device * TILES_DEV).astype(jnp.int32)
        values = lax.dynamic_slice_in_dim(tile_values, first_tile, TILES_DEV, 0).astype(jnp.float32)
        source = lax.dynamic_slice_in_dim(tile_source, first_tile, TILES_DEV, 0)
        target = lax.dynamic_slice_in_dim(tile_target, first_tile, TILES_DEV, 0)
        usable = jnp.arange(TILES_DEV, dtype=jnp.int32) < tile_count[device]
        picked = blocks[jnp.where(usable, source, 0)].astype(jnp.float32)
        product = jnp.einsum('tij,tjc->tic', values, picked, precision=lax.Precision.HIGHEST)
        product = jnp.where(usable[:, None, None], product, jnp.float32(0.0))
        running = jnp.zeros((RT_DEV, TILE, CHANNELS), jnp.float32).at[target].add(product)
        squares = jnp.where(usable[:, None], lax.optimization_barrier(jnp.sum(values * values, axis=2)), jnp.float32(0.0))
        row_norm = jnp.zeros((RT_DEV, TILE), jnp.float32).at[target].add(squares)
        return running * lax.rsqrt(1.0 + row_norm)[:, :, None]
    stacked_out = lax.map(per_device, jnp.arange(N_BLK, dtype=jnp.int32))
    return stacked_out.reshape(N_BLK * ROWS_DEV, CHANNELS)

def reference(features, tile_values, tile_source, tile_target, tile_count, weights, bias_vector):
    first_order = propagate(features, tile_values, tile_source, tile_target, tile_count).astype(jnp.bfloat16)
    second = propagate(first_order, tile_values, tile_source, tile_target, tile_count)
    second_order = (2.0 * second - features.astype(jnp.float32)).astype(jnp.bfloat16)
    result = jnp.dot(features, weights[0], preferred_element_type=jnp.float32)
    result = result + jnp.dot(first_order, weights[1], preferred_element_type=jnp.float32)
    result = result + jnp.dot(second_order, weights[2], preferred_element_type=jnp.float32)
    return (result + bias_vector[None, :]).astype(jnp.bfloat16)
```

```python
import functools

import jax
import jax.numpy as jnp
from jax import lax
from jax.experimental import pallas as pl
from jax.experimental.pallas import tpu as pltpu
from jax.sharding import PartitionSpec as P

MESH = pl.DeviceIdType.MESH
F32 = jnp.float32
BF16 = jnp.bfloat16
CHUNK = 16


def build_kernel(row_tiles, src, tgt, cnt, tiles_any, a_ref, inv_ref, tiles, sq, pos, sems):
    block = pl.program_id(0)
    slots = tiles_any.shape[0]
    tile = tiles_any.shape[1]
    chunks = slots // CHUNK

    def fetch(i):
        return pltpu.make_async_copy(
            tiles_any.at[pl.ds(i * CHUNK, CHUNK)], tiles.at[pl.ds(i * CHUNK, CHUNK)], sems.at[i]
        )

    @pl.when(block == 0)
    def _():
        for i in range(chunks):
            fetch(i).start()
        pos[0] = 0
        sq[...] = jnp.zeros_like(sq)

    a_ref[...] = jnp.zeros_like(a_ref)
    live = cnt[0]
    first = block * row_tiles
    last = first + row_tiles

    def go(k):
        return (k < live) & (src[jnp.minimum(k, slots - 1)] < last)

    def body(carry):
        k, _ = carry

        @pl.when(lax.rem(k, CHUNK) == 0)
        def _():
            fetch(lax.div(k, CHUNK)).wait()

        t = tgt[k]
        rows = pl.ds(pl.multiple_of(t * tile, tile), tile)
        cols = pl.ds(pl.multiple_of((src[k] - first) * tile, tile), tile)
        value = tiles[k].astype(F32)
        a_ref[0, rows, cols] = (a_ref[0, rows, cols].astype(F32) + value).astype(BF16)
        sq[t] = sq[t] + value * value
        return k + 1, go(k + 1)

    start = pos[0]
    end, _ = lax.while_loop(lambda c: c[1], body, (start, go(start)))
    pos[0] = end

    @pl.when(block == pl.num_programs(0) - 1)
    def _():
        for i in range(chunks):
            @pl.when(i * CHUNK >= end)
            def _():
                fetch(i).wait()
        for t in range(row_tiles):
            total = jnp.sum(sq[t], axis=1, keepdims=True)
            inv_ref[pl.ds(t * tile, tile), :] = jnp.broadcast_to(
                lax.rsqrt(1.0 + total), (tile, tile)
            )


def build(tile_values, tile_source, tile_target, tile_count, row_tiles, blocks):
    slots, tile, _ = tile_values.shape
    rows = row_tiles * tile
    return pl.pallas_call(
        functools.partial(build_kernel, row_tiles),
        grid_spec=pltpu.PrefetchScalarGridSpec(
            num_scalar_prefetch=3,
            grid=(blocks,),
            in_specs=[pl.BlockSpec(memory_space=pl.ANY)],
            out_specs=[
                pl.BlockSpec((1, rows, rows), lambda b, *_: (b, 0, 0)),
                pl.BlockSpec((rows, tile), lambda b, *_: (0, 0)),
            ],
            scratch_shapes=[
                pltpu.VMEM((slots, tile, tile), BF16),
                pltpu.VMEM((row_tiles, tile, tile), F32),
                pltpu.SMEM((1,), jnp.int32),
                pltpu.SemaphoreType.DMA((slots // CHUNK,)),
            ],
        ),
        out_shape=[
            jax.ShapeDtypeStruct((blocks, rows, rows), BF16),
            jax.ShapeDtypeStruct((rows, tile), F32),
        ],
        name="build",
    )(tile_source, tile_target, tile_count, tile_values)


def main_kernel(
    levels, f_ref, w_any, bias_ref, inv_ref, a_any, out_ref,
    fall, fld1, fld2, a_v, w_v, acc, base, fw1,
    asem, wsem, xs, xr, zs1, zr1, ys1, yr1, zs2, zr2, ys2, yr2,
):
    rt, tile = f_ref.shape[0], f_ref.shape[1]
    top = levels - 1
    me, mc = lax.axis_index("blk"), lax.axis_index("ch")
    z, y = lax.div(me, 2), lax.rem(me, 2)
    x, core = lax.div(mc, 2), lax.rem(mc, 2)
    partner = (me, 2 * x + (1 - core))
    across = (me, 2 * (1 - x) + core)
    y_dev = (2 * z + (1 - y), mc)
    z_dev = ((me + 2, mc), (me - 2, mc))
    can = (z < top, z > 0)

    for i in range(2 * levels):
        pltpu.make_async_copy(a_any.at[i], a_v.at[i], asem.at[i]).start()
    order_of = (mc, partner[1], across[1], 2 * (1 - x) + (1 - core))

    def w_copy(s, o):
        q = pl.multiple_of(order_of[s] * tile, tile)
        p = pl.multiple_of(mc * tile, tile)
        return pltpu.make_async_copy(
            w_any.at[o, pl.ds(q, tile), pl.ds(p, tile)],
            w_v.at[s, :, pl.ds(o * tile, tile)],
            wsem.at[s, o],
        )

    for s in range(4):
        for o in range(3):
            w_copy(s, o).start()

    barrier = pltpu.get_barrier_semaphore()
    for dev in (partner, across, y_dev):
        pl.semaphore_signal(barrier, inc=1, device_id=dev, device_id_type=MESH)
    for d in range(2):
        @pl.when(can[d])
        def _():
            pl.semaphore_signal(barrier, inc=1, device_id=z_dev[d], device_id_type=MESH)
    pl.semaphore_wait(barrier, 3 + can[0].astype(jnp.int32) + can[1].astype(jnp.int32))

    def remote(src, dst, ssem, rsem, dev):
        return pltpu.make_async_remote_copy(
            src_ref=src, dst_ref=dst, send_sem=ssem, recv_sem=rsem, device_id=dev, device_id_type=MESH
        )

    order = [rt - 1] + list(range(rt - 1))

    def x_copy(kind, c):
        src = f_ref.at[c] if kind < 2 else fall.at[1, c]
        return remote(
            src, fall.at[kind, c], xs.at[kind, c], xr.at[kind, c], across if kind == 1 else partner
        )

    for c in order:
        x_copy(1, c).start()
        x_copy(0, c).start()

    def z_view(fld, d, k, it):
        level = z - k if d == 0 else z + k
        return fld.at[2 * level + y, it] if it < rt else fld.at[2 * level + (1 - y), rt - 1]

    def z_copy(fld, zs, zr, d, k, it):
        view = z_view(fld, d, k, it)
        return remote(view, view, zs.at[d, k, it], zr.at[d, k, it], z_dev[d])

    def z_has(d, k):
        return z - k >= 0 if d == 0 else z + k <= top

    def y_index(d, k):
        return 0 if k == 0 else (1 + k - 1 if d == 0 else levels + k - 1)

    def y_copy(fld, ys, yr, d, k, it):
        level = z - k if d == 0 else z + k
        view = fld.at[2 * level + y, it]
        return remote(view, view, ys.at[y_index(d, k), it], yr.at[y_index(d, k), it], y_dev)

    def y_wait(fld, ys, yr, d, k, it):
        level = z - k if d == 0 else z + k
        view = fld.at[2 * level + (1 - y), it]
        remote(view, view, ys.at[y_index(d, k), it], yr.at[y_index(d, k), it], y_dev).wait_recv()

    def multiply(fld, block, fetch, init=False):
        if fetch:
            pltpu.make_async_copy(a_any.at[block], a_v.at[block], asem.at[block]).wait()
        half = rt * tile // 2
        rhs = fld[block].reshape(rt * tile, tile)

        @pl.loop(0, 2)
        def _(h):
            rows = pl.ds(pl.multiple_of(h * half, half), half)
            product = jnp.dot(a_v[block, rows, :], rhs, preferred_element_type=F32)
            acc[rows, :] = product if init else acc[rows, :] + product

    def emit_own(fld, sems, c):
        zs, zr, ys, yr = sems
        y_copy(fld, ys, yr, 0, 0, c).start()
        for d in range(2):
            @pl.when(can[d])
            def _():
                z_copy(fld, zs, zr, d, 0, c).start()

    def gather(fld, sems, fetch):
        zs, zr, ys, yr = sems
        y_wait(fld, ys, yr, 0, 0, rt - 1)
        for d in range(2):
            @pl.when(can[d])
            def _():
                z_copy(fld, zs, zr, d, 0, rt).start()
        multiply(fld, me, fetch, init=True)
        for k in range(1, levels):
            for it in order + [rt]:
                for d in range(2):
                    @pl.when(z_has(d, k))
                    def _():
                        remote(
                            z_view(fld, d, k, it), z_view(fld, d, k, it),
                            zs.at[d, k - 1, it], zr.at[d, k - 1, it], y_dev,
                        ).wait_recv()
                        if it < rt - 1:
                            y_copy(fld, ys, yr, d, k, it).start()
                        if k < top:
                            @pl.when(can[d])
                            def _():
                                z_copy(fld, zs, zr, d, k, it).start()
            if k == 1:
                for it in range(rt - 1):
                    y_wait(fld, ys, yr, 0, 0, it)
                multiply(fld, 2 * z + (1 - y), fetch)
            for d in range(2):
                @pl.when(z_has(d, k))
                def _():
                    level = z - k if d == 0 else z + k
                    multiply(fld, 2 * level + y, fetch)
                if k > 1:
                    other(fld, ys, yr, d, k - 1, fetch)
        for d in range(2):
            other(fld, ys, yr, d, top, fetch)

    def other(fld, ys, yr, d, k, fetch):
        @pl.when(z_has(d, k))
        def _():
            for it in range(rt - 1):
                y_wait(fld, ys, yr, d, k, it)
            level = z - k if d == 0 else z + k
            multiply(fld, 2 * level + (1 - y), fetch)

    def drain(fld, sems):
        zs, zr, ys, yr = sems
        for it in range(rt):
            y_copy(fld, ys, yr, 0, 0, it).wait_send()
        for d in range(2):
            for k in range(levels):
                @pl.when(z_has(d, k))
                def _():
                    if k > 0:
                        for it in range(rt - 1):
                            y_copy(fld, ys, yr, d, k, it).wait_send()
                    if k < top:
                        @pl.when(can[d])
                        def _():
                            for it in range(rt + 1):
                                z_copy(fld, zs, zr, d, k, it).wait_send()

    sems1 = (zs1, zr1, ys1, yr1)
    sems2 = (zs2, zr2, ys2, yr2)
    bias = bias_ref[:, pl.ds(pl.multiple_of(mc * tile, tile), tile)]
    for s in range(4):
        for o in range(3):
            w_copy(s, o).wait()

    for c in order:
        x_copy(1, c).wait_recv()
        x_copy(2, c).start()
        x_copy(0, c).wait_recv()
        r = jnp.dot(f_ref[c], w_v[0], preferred_element_type=F32)
        r += jnp.dot(fall[0, c], w_v[1], preferred_element_type=F32)
        r += jnp.dot(fall[1, c], w_v[2], preferred_element_type=F32)
        x_copy(2, c).wait_recv()
        r += jnp.dot(fall[2, c], w_v[3], preferred_element_type=F32)
        b2 = r[:, 2 * tile :]
        fld1[me, c] = b2.astype(BF16)
        emit_own(fld1, sems1, c)
        rows = pl.ds(c * tile, tile)
        base[rows, :] = r[:, :tile] - b2 + bias
        fw1[rows, :] = r[:, tile : 2 * tile]

    gather(fld1, sems1, True)
    for c in order:
        rows = pl.ds(c * tile, tile)
        fld2[me, c] = (fw1[rows, :] + 2.0 * (acc[rows, :] * inv_ref[rows, :])).astype(BF16)
        emit_own(fld2, sems2, c)
    gather(fld2, sems2, False)
    out_ref[...] = (base[...] + acc[...] * inv_ref[...]).astype(BF16)
    for kind in range(3):
        for c in range(rt):
            x_copy(kind, c).wait_send()
    drain(fld1, sems1)
    drain(fld2, sems2)


def fast(features, tile_values, tile_source, tile_target, tile_count, weights, bias_vector):
    tile = tile_values.shape[1]
    rows, cols = features.shape
    rt = rows // tile
    blocks = lax.axis_size("blk")
    levels = blocks // 2
    a, inv = build(tile_values, tile_source, tile_target, tile_count, rt, blocks)
    vmem = pl.BlockSpec(memory_space=pltpu.VMEM)
    hbm = pl.BlockSpec(memory_space=pl.ANY)
    dma = pltpu.SemaphoreType.DMA
    gather_sems = [
        dma((2, levels - 1, rt + 1)), dma((2, levels - 1, rt + 1)),
        dma((2 * levels - 1, rt)), dma((2 * levels - 1, rt)),
    ]
    return pl.pallas_call(
        functools.partial(main_kernel, levels),
        out_shape=jax.ShapeDtypeStruct((rows, cols), BF16),
        in_specs=[vmem, hbm, vmem, vmem, hbm],
        out_specs=vmem,
        scratch_shapes=[
            pltpu.VMEM((3, rt, tile, tile), BF16),
            pltpu.VMEM((blocks, rt, tile, tile), BF16),
            pltpu.VMEM((blocks, rt, tile, tile), BF16),
            pltpu.VMEM((blocks, rows, rows), BF16),
            pltpu.VMEM((4, tile, 3 * tile), BF16),
            pltpu.VMEM((rows, tile), F32),
            pltpu.VMEM((rows, tile), F32),
            pltpu.VMEM((rows, tile), F32),
            dma((blocks,)),
            dma((4, 3)),
            dma((3, rt)),
            dma((3, rt)),
        ] + gather_sems + gather_sems,
        compiler_params=pltpu.CompilerParams(collective_id=0, has_side_effects=True),
        name="propagate",
    )(features.reshape(rt, tile, cols), weights, bias_vector.reshape(1, -1), inv, a)


def per_device(features, tile_values, tile_source, tile_target, tile_count, weights, bias_vector):
    tile_size = tile_values.shape[1]
    slot_total = tile_values.shape[0]
    channels = features.shape[1]
    row_tiles = features.shape[0] // tile_size
    block_rows = row_tiles * tile_size
    block_count = lax.axis_size("blk")
    slot_cap = max(2, (2 * slot_total + block_count - 1) // block_count)
    usable = jnp.arange(slot_total, dtype=jnp.int32) < tile_count[0]
    squares = jnp.einsum(
        "tij,tij->ti", tile_values, tile_values, preferred_element_type=jnp.float32
    )
    squares = jnp.where(usable[:, None], squares, 0.0)
    onehot = (
        (tile_target[:, None] == jnp.arange(row_tiles, dtype=jnp.int32)[None, :]) & usable[:, None]
    ).astype(jnp.float32)
    row_norm = jnp.dot(onehot.T, squares, precision=lax.Precision.HIGHEST)
    inverse = lax.rsqrt(1.0 + row_norm).reshape(-1)
    zero_sum = jnp.zeros((row_tiles, tile_size, channels), jnp.float32)

    def cycle_prop(signal):
        segment = lax.all_gather(signal, "blk", axis=0, tiled=True)
        offset = jnp.int32(0)
        count_rows = segment.shape[0]
        window = min(slot_total, slot_cap * (count_rows // block_rows + 2))
        low_row = tile_source * tile_size
        first_slot = jnp.sum(usable & (low_row + tile_size <= offset))
        end_slot = jnp.sum(usable & (low_row < offset + count_rows))
        start_slot = jnp.minimum(first_slot, slot_total - window)
        slot_ids = start_slot + jnp.arange(window, dtype=jnp.int32)
        in_range = (slot_ids >= first_slot) & (slot_ids < end_slot)
        row_ids = tile_source[:, None] * tile_size + jnp.arange(tile_size, dtype=jnp.int32)[None, :]
        inside = (row_ids >= 0) & (row_ids < count_rows) & in_range[:, None]
        picked = jnp.take(segment, jnp.clip(row_ids, 0, count_rows - 1).reshape(-1), axis=0)
        picked = picked.reshape(window, tile_size, channels)
        picked = jnp.where(inside[:, :, None], picked, jnp.zeros((), segment.dtype))
        product = jnp.einsum(
            "gij,gjc->gic", tile_values, picked, preferred_element_type=jnp.float32
        )
        product = jnp.where(in_range[:, None, None], product, 0.0)
        summed = zero_sum.at[tile_target].add(product)
        return summed.reshape(-1, channels) * inverse[:, None]

    col_start = lax.axis_index("ch") * channels
    bias_part = lax.dynamic_slice_in_dim(bias_vector, col_start, channels, 0)
    w_cols = lax.dynamic_slice_in_dim(weights, col_start, channels, 2)

    def mix_term(order_term, order_index, running):
        w_slice = w_cols[order_index]
        return running + jnp.dot(
            lax.all_gather(order_term, "ch", axis=1, tiled=True),
            w_slice,
            preferred_element_type=jnp.float32,
        )

    result = mix_term(features, 0, jnp.zeros((features.shape[0], channels), jnp.float32))
    first_order = cycle_prop(features).astype(jnp.bfloat16)
    result = mix_term(first_order, 1, result)
    second_order = (2.0 * cycle_prop(first_order) - features.astype(jnp.float32)).astype(
        jnp.bfloat16
    )
    result = mix_term(second_order, 2, result)
    return (result + bias_part[None, :]).astype(jnp.bfloat16)


def solution(mesh):
    dense = mesh.shape["blk"] == 8 and mesh.shape["ch"] == 4
    return jax.shard_map(
        fast if dense else per_device,
        mesh=mesh,
        in_specs=(P("blk", "ch"), P("blk", None, None), P("blk"), P("blk"), P("blk"), P(), P()),
        out_specs=P("blk", "ch"),
        check_vma=False,
    )
```

```python
import functools

import jax
import jax.numpy as jnp
from jax import lax
from jax.experimental import pallas as pl
from jax.experimental.pallas import tpu as pltpu
from jax.sharding import PartitionSpec as P

MESH = pl.DeviceIdType.MESH
F32 = jnp.float32
BF16 = jnp.bfloat16


def merge_kernel(
    row_tiles, src, tgt, cnt, tiles_any, idx, extra_any, got, total, packed, slot_group, insem, outsem
):
    slots = tiles_any.shape[0]
    empty = slots + extra_any.shape[0]

    @pl.loop(0, idx.shape[0] // 8)
    def _(p):
        for q in range(8):
            idx[p * 8 + q] = empty

    def fetch(slot, entry):
        return pltpu.make_async_copy(tiles_any.at[slot], got.at[entry], insem.at[entry])

    def scan(k, carry):
        place = src[k] * row_tiles + tgt[k]
        held = idx[place]
        groups, entries = carry

        @pl.when(held == empty)
        def _():
            idx[place] = k

        fresh = held < slots
        again = held < empty

        @pl.when(fresh)
        def _():
            idx[place] = slots + groups
            fetch(held, entries).start()
            slot_group[entries] = groups

        step = fresh.astype(jnp.int32)

        @pl.when(again)
        def _():
            fetch(k, entries + step).start()
            slot_group[entries + step] = jnp.where(fresh, groups, held - slots)

        return groups + step, entries + step + again.astype(jnp.int32)

    groups, entries = lax.fori_loop(0, cnt[0], scan, (jnp.int32(0), jnp.int32(0)))

    @pl.loop(0, groups)
    def _(g):
        total[g] = jnp.zeros_like(total[g])

    @pl.loop(0, entries)
    def _(e):
        fetch(0, e).wait()
        g = slot_group[e]
        total[g] = total[g] + got[e].astype(F32)

    def put(g):
        return pltpu.make_async_copy(packed.at[g], extra_any.at[g], outsem.at[g])

    @pl.loop(0, groups)
    def _(g):
        packed[g] = total[g].astype(BF16)
        put(g).start()

    @pl.loop(0, groups)
    def _(g):
        put(g).wait()


def merge(tile_values, tile_source, tile_target, tile_count, row_tiles, blocks):
    slots, tile, _ = tile_values.shape
    smem = pl.BlockSpec(memory_space=pltpu.SMEM)
    hbm = pl.BlockSpec(memory_space=pl.ANY)
    groups = slots // 2
    return pl.pallas_call(
        functools.partial(merge_kernel, row_tiles),
        in_specs=[smem, smem, smem, hbm],
        out_specs=[smem, hbm],
        scratch_shapes=[
            pltpu.VMEM((slots, tile, tile), BF16),
            pltpu.VMEM((groups, tile, tile), F32),
            pltpu.VMEM((groups, tile, tile), BF16),
            pltpu.SMEM((slots,), jnp.int32),
            pltpu.SemaphoreType.DMA((slots,)),
            pltpu.SemaphoreType.DMA((groups,)),
        ],
        out_shape=[
            jax.ShapeDtypeStruct((blocks * row_tiles * row_tiles,), jnp.int32),
            jax.ShapeDtypeStruct((groups, tile, tile), BF16),
        ],
        name="merge",
    )(tile_source, tile_target, tile_count, tile_values)


def main_kernel(
    levels, f_any, w_any, bias_ref, tgt, cnt, idx, tiles_any, extra_any, out_ref,
    f_ref, fall, fld1, fld2, a_v, tiles, w_v, acc, base, fw1, inv_ref,
    fsem, asem, wsem, xs, xr, zs1, zr1, ys1, yr1, zs2, zr2, ys2, yr2,
):
    rt, tile = f_any.shape[0], f_any.shape[1]
    top = levels - 1
    me, mc = lax.axis_index("blk"), lax.axis_index("ch")
    z, y = lax.div(me, 2), lax.rem(me, 2)
    x, core = lax.div(mc, 2), lax.rem(mc, 2)
    partner = (me, 2 * x + (1 - core))
    across = (me, 2 * (1 - x) + core)
    y_dev = (2 * z + (1 - y), mc)
    z_dev = ((me + 2, mc), (me - 2, mc))
    can = (z < top, z > 0)

    barrier = pltpu.get_barrier_semaphore()
    for dev in (partner, across, y_dev):
        pl.semaphore_signal(barrier, inc=1, device_id=dev, device_id_type=MESH)
    for d in range(2):
        @pl.when(can[d])
        def _():
            pl.semaphore_signal(barrier, inc=1, device_id=z_dev[d], device_id_type=MESH)

    slots, extras = tiles_any.shape[0], extra_any.shape[0]

    def f_copy(c):
        return pltpu.make_async_copy(f_any.at[c], f_ref.at[c], fsem.at[c])

    for c in [rt - 1] + list(range(rt - 1)):
        f_copy(c).start()
    order_of = (mc, partner[1], across[1], 2 * (1 - x) + (1 - core))

    def w_copy(s, o):
        q = pl.multiple_of(order_of[s] * tile, tile)
        p = pl.multiple_of(mc * tile, tile)
        return pltpu.make_async_copy(
            w_any.at[o, pl.ds(q, tile), pl.ds(p, tile)],
            w_v.at[s, :, pl.ds(o * tile, tile)],
            wsem.at[s, o],
        )

    for s in range(4):
        for o in range(3):
            w_copy(s, o).start()

    pl.semaphore_wait(barrier, 3 + can[0].astype(jnp.int32) + can[1].astype(jnp.int32))

    def remote(src, dst, ssem, rsem, dev):
        return pltpu.make_async_remote_copy(
            src_ref=src, dst_ref=dst, send_sem=ssem, recv_sem=rsem, device_id=dev, device_id_type=MESH
        )

    order = [rt - 1] + list(range(rt - 1))

    def x_copy(kind, c):
        src = f_any.at[c] if kind < 2 else fall.at[1, c]
        return remote(
            src, fall.at[kind, c], xs.at[kind, c], xr.at[kind, c], across if kind == 1 else partner
        )

    for c in order:
        x_copy(1, c).start()
        x_copy(0, c).start()
    tile_copies = (
        pltpu.make_async_copy(tiles_any, tiles.at[pl.ds(0, slots)], asem.at[0]),
        pltpu.make_async_copy(extra_any, tiles.at[pl.ds(slots, extras)], asem.at[1]),
    )
    for copy in tile_copies:
        copy.start()
    tiles[slots + extras] = jnp.zeros((tile, tile), BF16)

    def z_view(fld, d, k, it):
        level = z - k if d == 0 else z + k
        return fld.at[2 * level + y, it] if it < rt else fld.at[2 * level + (1 - y), rt - 1]

    def z_copy(fld, zs, zr, d, k, it):
        view = z_view(fld, d, k, it)
        return remote(view, view, zs.at[d, k, it], zr.at[d, k, it], z_dev[d])

    def z_has(d, k):
        return z - k >= 0 if d == 0 else z + k <= top

    def y_index(d, k):
        return 0 if k == 0 else (1 + k - 1 if d == 0 else levels + k - 1)

    def y_copy(fld, ys, yr, d, k, it):
        level = z - k if d == 0 else z + k
        view = fld.at[2 * level + y, it]
        return remote(view, view, ys.at[y_index(d, k), it], yr.at[y_index(d, k), it], y_dev)

    def y_wait(fld, ys, yr, d, k, it):
        level = z - k if d == 0 else z + k
        view = fld.at[2 * level + (1 - y), it]
        remote(view, view, ys.at[y_index(d, k), it], yr.at[y_index(d, k), it], y_dev).wait_recv()

    def fill(block):
        @pl.loop(0, rt)
        def _(t):
            for j in range(rt):
                a_v[block, pl.ds(pl.multiple_of(t * tile, tile), tile), pl.ds(j * tile, tile)] = (
                    tiles[idx[(block * rt + j) * rt + t]]
                )

    def norms():
        part = 32
        for r in range(tile // part):
            def add(k, sums):
                value = tiles[k, pl.ds(r * part, part), :].astype(F32)
                value = value * value
                aim = jnp.where(k < cnt[0], tgt[k], rt)
                return tuple(
                    sums[t] + value * jnp.where(aim == t, 1.0, 0.0).astype(F32) for t in range(rt)
                )

            zero = jnp.zeros((part, tile), F32)
            sums = lax.fori_loop(0, slots, add, (zero,) * rt)
            for t in range(rt):
                total = jnp.sum(sums[t], axis=1, keepdims=True)
                inv_ref[pl.ds(t * tile + r * part, part), :] = jnp.broadcast_to(
                    lax.rsqrt(1.0 + total), (part, tile)
                )

    def multiply(fld, block, fetch, init=False):
        if fetch:
            fill(block)
        half = rt * tile // 2
        rhs = fld[block].reshape(rt * tile, tile)

        @pl.loop(0, 2)
        def _(h):
            rows = pl.ds(pl.multiple_of(h * half, half), half)
            product = jnp.dot(a_v[block, rows, :], rhs, preferred_element_type=F32)
            acc[rows, :] = product if init else acc[rows, :] + product

    def emit_own(fld, sems, c):
        zs, zr, ys, yr = sems
        y_copy(fld, ys, yr, 0, 0, c).start()
        for d in range(2):
            @pl.when(can[d])
            def _():
                z_copy(fld, zs, zr, d, 0, c).start()

    def gather(fld, sems, fetch):
        zs, zr, ys, yr = sems
        y_wait(fld, ys, yr, 0, 0, rt - 1)
        for d in range(2):
            @pl.when(can[d])
            def _():
                z_copy(fld, zs, zr, d, 0, rt).start()
        if fetch:
            for copy in tile_copies:
                copy.wait()
            norms()
        multiply(fld, me, fetch, init=True)
        for k in range(1, levels):
            for it in order + [rt]:
                for d in range(2):
                    @pl.when(z_has(d, k))
                    def _():
                        remote(
                            z_view(fld, d, k, it), z_view(fld, d, k, it),
                            zs.at[d, k - 1, it], zr.at[d, k - 1, it], y_dev,
                        ).wait_recv()
                        if it < rt - 1:
                            y_copy(fld, ys, yr, d, k, it).start()
                        if k < top:
                            @pl.when(can[d])
                            def _():
                                z_copy(fld, zs, zr, d, k, it).start()
            if k == 1:
                for it in range(rt - 1):
                    y_wait(fld, ys, yr, 0, 0, it)
                multiply(fld, 2 * z + (1 - y), fetch)
            for d in range(2):
                @pl.when(z_has(d, k))
                def _():
                    level = z - k if d == 0 else z + k
                    multiply(fld, 2 * level + y, fetch)
                if k > 1:
                    other(fld, ys, yr, d, k - 1, fetch)
        for d in range(2):
            other(fld, ys, yr, d, top, fetch)

    def other(fld, ys, yr, d, k, fetch):
        @pl.when(z_has(d, k))
        def _():
            for it in range(rt - 1):
                y_wait(fld, ys, yr, d, k, it)
            level = z - k if d == 0 else z + k
            multiply(fld, 2 * level + (1 - y), fetch)

    def drain(fld, sems):
        zs, zr, ys, yr = sems
        for it in range(rt):
            y_copy(fld, ys, yr, 0, 0, it).wait_send()
        for d in range(2):
            for k in range(levels):
                @pl.when(z_has(d, k))
                def _():
                    if k > 0:
                        for it in range(rt - 1):
                            y_copy(fld, ys, yr, d, k, it).wait_send()
                    if k < top:
                        @pl.when(can[d])
                        def _():
                            for it in range(rt + 1):
                                z_copy(fld, zs, zr, d, k, it).wait_send()

    sems1 = (zs1, zr1, ys1, yr1)
    sems2 = (zs2, zr2, ys2, yr2)
    bias = bias_ref[:, pl.ds(pl.multiple_of(mc * tile, tile), tile)]
    for s in range(4):
        for o in range(3):
            w_copy(s, o).wait()

    for c in order:
        x_copy(1, c).wait_recv()
        x_copy(2, c).start()
        f_copy(c).wait()
        x_copy(0, c).wait_recv()
        r = jnp.dot(f_ref[c], w_v[0], preferred_element_type=F32)
        r += jnp.dot(fall[0, c], w_v[1], preferred_element_type=F32)
        r += jnp.dot(fall[1, c], w_v[2], preferred_element_type=F32)
        x_copy(2, c).wait_recv()
        r += jnp.dot(fall[2, c], w_v[3], preferred_element_type=F32)
        b2 = r[:, 2 * tile :]
        fld1[me, c] = b2.astype(BF16)
        emit_own(fld1, sems1, c)
        rows = pl.ds(c * tile, tile)
        base[rows, :] = r[:, :tile] - b2 + bias
        fw1[rows, :] = r[:, tile : 2 * tile]

    gather(fld1, sems1, True)
    for c in order:
        rows = pl.ds(c * tile, tile)
        fld2[me, c] = (fw1[rows, :] + 2.0 * (acc[rows, :] * inv_ref[rows, :])).astype(BF16)
        emit_own(fld2, sems2, c)
    gather(fld2, sems2, False)
    out_ref[...] = (base[...] + acc[...] * inv_ref[...]).astype(BF16)
    for kind in range(3):
        for c in range(rt):
            x_copy(kind, c).wait_send()
    drain(fld1, sems1)
    drain(fld2, sems2)


def fast(features, tile_values, tile_source, tile_target, tile_count, weights, bias_vector):
    tile = tile_values.shape[1]
    rows, cols = features.shape
    rt = rows // tile
    blocks = lax.axis_size("blk")
    levels = blocks // 2
    idx, extra = merge(tile_values, tile_source, tile_target, tile_count, rt, blocks)
    vmem = pl.BlockSpec(memory_space=pltpu.VMEM)
    hbm = pl.BlockSpec(memory_space=pl.ANY)
    smem = pl.BlockSpec(memory_space=pltpu.SMEM)
    slots = tile_values.shape[0]
    dma = pltpu.SemaphoreType.DMA
    gather_sems = [
        dma((2, levels - 1, rt + 1)), dma((2, levels - 1, rt + 1)),
        dma((2 * levels - 1, rt)), dma((2 * levels - 1, rt)),
    ]
    return pl.pallas_call(
        functools.partial(main_kernel, levels),
        out_shape=jax.ShapeDtypeStruct((rows, cols), BF16),
        in_specs=[hbm, hbm, vmem, smem, smem, smem, hbm, hbm],
        out_specs=vmem,
        scratch_shapes=[
            pltpu.VMEM((rt, tile, tile), BF16),
            pltpu.VMEM((3, rt, tile, tile), BF16),
            pltpu.VMEM((blocks, rt, tile, tile), BF16),
            pltpu.VMEM((blocks, rt, tile, tile), BF16),
            pltpu.VMEM((blocks, rows, rows), BF16),
            pltpu.VMEM((slots + slots // 2 + 1, tile, tile), BF16),
            pltpu.VMEM((4, tile, 3 * tile), BF16),
            pltpu.VMEM((rows, tile), F32),
            pltpu.VMEM((rows, tile), F32),
            pltpu.VMEM((rows, tile), F32),
            pltpu.VMEM((rows, tile), F32),
            dma((rt,)),
            dma((2,)),
            dma((4, 3)),
            dma((3, rt)),
            dma((3, rt)),
        ] + gather_sems + gather_sems,
        compiler_params=pltpu.CompilerParams(collective_id=0, has_side_effects=True),
        name="propagate",
    )(features.reshape(rt, tile, cols), weights, bias_vector.reshape(1, -1),
      tile_target, tile_count, idx, tile_values, extra)


def per_device(features, tile_values, tile_source, tile_target, tile_count, weights, bias_vector):
    tile_size = tile_values.shape[1]
    slot_total = tile_values.shape[0]
    channels = features.shape[1]
    row_tiles = features.shape[0] // tile_size
    block_rows = row_tiles * tile_size
    block_count = lax.axis_size("blk")
    slot_cap = max(2, (2 * slot_total + block_count - 1) // block_count)
    usable = jnp.arange(slot_total, dtype=jnp.int32) < tile_count[0]
    squares = jnp.einsum(
        "tij,tij->ti", tile_values, tile_values, preferred_element_type=jnp.float32
    )
    squares = jnp.where(usable[:, None], squares, 0.0)
    onehot = (
        (tile_target[:, None] == jnp.arange(row_tiles, dtype=jnp.int32)[None, :]) & usable[:, None]
    ).astype(jnp.float32)
    row_norm = jnp.dot(onehot.T, squares, precision=lax.Precision.HIGHEST)
    inverse = lax.rsqrt(1.0 + row_norm).reshape(-1)
    zero_sum = jnp.zeros((row_tiles, tile_size, channels), jnp.float32)

    def cycle_prop(signal):
        segment = lax.all_gather(signal, "blk", axis=0, tiled=True)
        offset = jnp.int32(0)
        count_rows = segment.shape[0]
        window = min(slot_total, slot_cap * (count_rows // block_rows + 2))
        low_row = tile_source * tile_size
        first_slot = jnp.sum(usable & (low_row + tile_size <= offset))
        end_slot = jnp.sum(usable & (low_row < offset + count_rows))
        start_slot = jnp.minimum(first_slot, slot_total - window)
        slot_ids = start_slot + jnp.arange(window, dtype=jnp.int32)
        in_range = (slot_ids >= first_slot) & (slot_ids < end_slot)
        row_ids = tile_source[:, None] * tile_size + jnp.arange(tile_size, dtype=jnp.int32)[None, :]
        inside = (row_ids >= 0) & (row_ids < count_rows) & in_range[:, None]
        picked = jnp.take(segment, jnp.clip(row_ids, 0, count_rows - 1).reshape(-1), axis=0)
        picked = picked.reshape(window, tile_size, channels)
        picked = jnp.where(inside[:, :, None], picked, jnp.zeros((), segment.dtype))
        product = jnp.einsum(
            "gij,gjc->gic", tile_values, picked, preferred_element_type=jnp.float32
        )
        product = jnp.where(in_range[:, None, None], product, 0.0)
        summed = zero_sum.at[tile_target].add(product)
        return summed.reshape(-1, channels) * inverse[:, None]

    col_start = lax.axis_index("ch") * channels
    bias_part = lax.dynamic_slice_in_dim(bias_vector, col_start, channels, 0)
    w_cols = lax.dynamic_slice_in_dim(weights, col_start, channels, 2)

    def mix_term(order_term, order_index, running):
        w_slice = w_cols[order_index]
        return running + jnp.dot(
            lax.all_gather(order_term, "ch", axis=1, tiled=True),
            w_slice,
            preferred_element_type=jnp.float32,
        )

    result = mix_term(features, 0, jnp.zeros((features.shape[0], channels), jnp.float32))
    first_order = cycle_prop(features).astype(jnp.bfloat16)
    result = mix_term(first_order, 1, result)
    second_order = (2.0 * cycle_prop(first_order) - features.astype(jnp.float32)).astype(
        jnp.bfloat16
    )
    result = mix_term(second_order, 2, result)
    return (result + bias_part[None, :]).astype(jnp.bfloat16)


def solution(mesh):
    dense = mesh.shape["blk"] == 8 and mesh.shape["ch"] == 4
    return jax.shard_map(
        fast if dense else per_device,
        mesh=mesh,
        in_specs=(P("blk", "ch"), P("blk", None, None), P("blk"), P("blk"), P("blk"), P(), P()),
        out_specs=P("blk", "ch"),
        check_vma=False,
    )
```

```python
import functools

import jax
import jax.numpy as jnp
from jax import lax
from jax.experimental import pallas as pl
from jax.experimental.pallas import tpu as pltpu
from jax.sharding import PartitionSpec as P

MESH = pl.DeviceIdType.MESH
F32 = jnp.float32
BF16 = jnp.bfloat16
CHUNK = 16


def build_kernel(row_tiles, src, tgt, cnt, tiles_any, a_ref, inv_ref, tiles, sq, pos, sems):
    block = pl.program_id(0)
    slots = tiles_any.shape[0]
    tile = tiles_any.shape[1]
    chunks = slots // CHUNK

    def fetch(i):
        return pltpu.make_async_copy(
            tiles_any.at[pl.ds(i * CHUNK, CHUNK)], tiles.at[pl.ds(i * CHUNK, CHUNK)], sems.at[i]
        )

    @pl.when(block == 0)
    def _():
        for i in range(chunks):
            fetch(i).start()
        pos[0] = 0
        sq[...] = jnp.zeros_like(sq)

    a_ref[...] = jnp.zeros_like(a_ref)
    live = cnt[0]
    first = block * row_tiles
    last = first + row_tiles

    def go(k):
        return (k < live) & (src[jnp.minimum(k, slots - 1)] < last)

    def body(carry):
        k, _ = carry

        @pl.when(lax.rem(k, CHUNK) == 0)
        def _():
            fetch(lax.div(k, CHUNK)).wait()

        t = tgt[k]
        rows = pl.ds(pl.multiple_of(t * tile, tile), tile)
        cols = pl.ds(pl.multiple_of((src[k] - first) * tile, tile), tile)
        value = tiles[k].astype(F32)
        a_ref[0, rows, cols] = (a_ref[0, rows, cols].astype(F32) + value).astype(BF16)
        sq[t] = sq[t] + value * value
        return k + 1, go(k + 1)

    start = pos[0]
    end, _ = lax.while_loop(lambda c: c[1], body, (start, go(start)))
    pos[0] = end

    @pl.when(block == pl.num_programs(0) - 1)
    def _():
        for i in range(chunks):
            @pl.when(i * CHUNK >= end)
            def _():
                fetch(i).wait()
        for t in range(row_tiles):
            total = jnp.sum(sq[t], axis=1, keepdims=True)
            inv_ref[pl.ds(t * tile, tile), :] = jnp.broadcast_to(
                lax.rsqrt(1.0 + total), (tile, tile)
            )


def build(tile_values, tile_source, tile_target, tile_count, row_tiles, blocks):
    slots, tile, _ = tile_values.shape
    rows = row_tiles * tile
    return pl.pallas_call(
        functools.partial(build_kernel, row_tiles),
        grid_spec=pltpu.PrefetchScalarGridSpec(
            num_scalar_prefetch=3,
            grid=(blocks,),
            in_specs=[pl.BlockSpec(memory_space=pltpu.HBM)],
            out_specs=[
                pl.BlockSpec((1, rows, rows), lambda b, *_: (b, 0, 0)),
                pl.BlockSpec((rows, tile), lambda b, *_: (0, 0)),
            ],
            scratch_shapes=[
                pltpu.VMEM((slots, tile, tile), BF16),
                pltpu.VMEM((row_tiles, tile, tile), F32),
                pltpu.SMEM((1,), jnp.int32),
                pltpu.SemaphoreType.DMA((slots // CHUNK,)),
            ],
        ),
        out_shape=[
            jax.ShapeDtypeStruct((blocks, rows, rows), BF16),
            jax.ShapeDtypeStruct((rows, tile), F32),
        ],
        compiler_params=pltpu.CompilerParams(vmem_limit_bytes=24 << 20),
        name="build",
    )(tile_source, tile_target, tile_count, tile_values)


def main_kernel(
    levels, f_ref, w_any, bias_ref, inv_ref, a_any, out_ref,
    fall, fld1, fld2, a_v, w_v, acc, base, fw1,
    asem, wsem, xs, xr, zs1, zr1, ys1, yr1, zs2, zr2, ys2, yr2,
):
    rt, tile = f_ref.shape[0], f_ref.shape[1]
    top = levels - 1
    me, mc = lax.axis_index("blk"), lax.axis_index("ch")
    z, y = lax.div(me, 2), lax.rem(me, 2)
    x, core = lax.div(mc, 2), lax.rem(mc, 2)
    partner = (me, 2 * x + (1 - core))
    across = (me, 2 * (1 - x) + core)
    y_dev = (2 * z + (1 - y), mc)
    z_dev = ((me + 2, mc), (me - 2, mc))
    can = (z < top, z > 0)

    for i in range(2 * levels):
        pltpu.make_async_copy(a_any.at[i], a_v.at[i], asem.at[i]).start()
    order_of = (mc, partner[1], across[1], 2 * (1 - x) + (1 - core))

    def w_copy(s, o):
        q = pl.multiple_of(order_of[s] * tile, tile)
        p = pl.multiple_of(mc * tile, tile)
        return pltpu.make_async_copy(
            w_any.at[o, pl.ds(q, tile), pl.ds(p, tile)],
            w_v.at[s, :, pl.ds(o * tile, tile)],
            wsem.at[s, o],
        )

    for s in range(4):
        for o in range(3):
            w_copy(s, o).start()

    barrier = pltpu.get_barrier_semaphore()
    for dev in (partner, across, y_dev):
        pl.semaphore_signal(barrier, inc=1, device_id=dev, device_id_type=MESH)
    for d in range(2):
        @pl.when(can[d])
        def _():
            pl.semaphore_signal(barrier, inc=1, device_id=z_dev[d], device_id_type=MESH)
    pl.semaphore_wait(barrier, 3 + can[0].astype(jnp.int32) + can[1].astype(jnp.int32))

    def remote(src, dst, ssem, rsem, dev):
        return pltpu.make_async_remote_copy(
            src_ref=src, dst_ref=dst, send_sem=ssem, recv_sem=rsem, device_id=dev, device_id_type=MESH
        )

    order = [rt - 1] + list(range(rt - 1))

    def x_copy(kind, c):
        src = f_ref.at[c] if kind < 2 else fall.at[1, c]
        return remote(
            src, fall.at[kind, c], xs.at[kind, c], xr.at[kind, c], across if kind == 1 else partner
        )

    for c in order:
        x_copy(1, c).start()
        x_copy(0, c).start()

    def z_view(fld, d, k, it):
        level = z - k if d == 0 else z + k
        return fld.at[2 * level + y, it] if it < rt else fld.at[2 * level + (1 - y), rt - 1]

    def z_copy(fld, zs, zr, d, k, it):
        view = z_view(fld, d, k, it)
        return remote(view, view, zs.at[d, k, it], zr.at[d, k, it], z_dev[d])

    def z_has(d, k):
        return z - k >= 0 if d == 0 else z + k <= top

    def y_index(d, k):
        return 0 if k == 0 else (1 + k - 1 if d == 0 else levels + k - 1)

    def y_copy(fld, ys, yr, d, k, it):
        level = z - k if d == 0 else z + k
        view = fld.at[2 * level + y, it]
        return remote(view, view, ys.at[y_index(d, k), it], yr.at[y_index(d, k), it], y_dev)

    def y_wait(fld, ys, yr, d, k, it):
        level = z - k if d == 0 else z + k
        view = fld.at[2 * level + (1 - y), it]
        remote(view, view, ys.at[y_index(d, k), it], yr.at[y_index(d, k), it], y_dev).wait_recv()

    def multiply(fld, block, fetch, init=False):
        if fetch:
            pltpu.make_async_copy(a_any.at[block], a_v.at[block], asem.at[block]).wait()
        half = rt * tile // 2
        rhs = fld[block].reshape(rt * tile, tile)

        @pl.loop(0, 2)
        def _(h):
            rows = pl.ds(pl.multiple_of(h * half, half), half)
            product = jnp.dot(a_v[block, rows, :], rhs, preferred_element_type=F32)
            acc[rows, :] = product if init else acc[rows, :] + product

    def emit_own(fld, sems, c):
        zs, zr, ys, yr = sems
        y_copy(fld, ys, yr, 0, 0, c).start()
        for d in range(2):
            @pl.when(can[d])
            def _():
                z_copy(fld, zs, zr, d, 0, c).start()

    def gather(fld, sems, fetch):
        zs, zr, ys, yr = sems
        y_wait(fld, ys, yr, 0, 0, rt - 1)
        for d in range(2):
            @pl.when(can[d])
            def _():
                z_copy(fld, zs, zr, d, 0, rt).start()
        multiply(fld, me, fetch, init=True)
        for k in range(1, levels):
            for it in order + [rt]:
                for d in range(2):
                    @pl.when(z_has(d, k))
                    def _():
                        remote(
                            z_view(fld, d, k, it), z_view(fld, d, k, it),
                            zs.at[d, k - 1, it], zr.at[d, k - 1, it], y_dev,
                        ).wait_recv()
                        if it < rt - 1:
                            y_copy(fld, ys, yr, d, k, it).start()
                        if k < top:
                            @pl.when(can[d])
                            def _():
                                z_copy(fld, zs, zr, d, k, it).start()
            if k == 1:
                for it in range(rt - 1):
                    y_wait(fld, ys, yr, 0, 0, it)
                multiply(fld, 2 * z + (1 - y), fetch)
            for d in range(2):
                @pl.when(z_has(d, k))
                def _():
                    level = z - k if d == 0 else z + k
                    multiply(fld, 2 * level + y, fetch)
                if k > 1:
                    other(fld, ys, yr, d, k - 1, fetch)
        for d in range(2):
            other(fld, ys, yr, d, top, fetch)

    def other(fld, ys, yr, d, k, fetch):
        @pl.when(z_has(d, k))
        def _():
            for it in range(rt - 1):
                y_wait(fld, ys, yr, d, k, it)
            level = z - k if d == 0 else z + k
            multiply(fld, 2 * level + (1 - y), fetch)

    def drain(fld, sems):
        zs, zr, ys, yr = sems
        for it in range(rt):
            y_copy(fld, ys, yr, 0, 0, it).wait_send()
        for d in range(2):
            for k in range(levels):
                @pl.when(z_has(d, k))
                def _():
                    if k > 0:
                        for it in range(rt - 1):
                            y_copy(fld, ys, yr, d, k, it).wait_send()
                    if k < top:
                        @pl.when(can[d])
                        def _():
                            for it in range(rt + 1):
                                z_copy(fld, zs, zr, d, k, it).wait_send()

    sems1 = (zs1, zr1, ys1, yr1)
    sems2 = (zs2, zr2, ys2, yr2)
    bias = bias_ref[:, pl.ds(pl.multiple_of(mc * tile, tile), tile)]
    for s in range(4):
        for o in range(3):
            w_copy(s, o).wait()

    for c in order:
        x_copy(1, c).wait_recv()
        x_copy(2, c).start()
        x_copy(0, c).wait_recv()
        r = jnp.dot(f_ref[c], w_v[0], preferred_element_type=F32)
        r += jnp.dot(fall[0, c], w_v[1], preferred_element_type=F32)
        r += jnp.dot(fall[1, c], w_v[2], preferred_element_type=F32)
        x_copy(2, c).wait_recv()
        r += jnp.dot(fall[2, c], w_v[3], preferred_element_type=F32)
        b2 = r[:, 2 * tile :]
        fld1[me, c] = b2.astype(BF16)
        emit_own(fld1, sems1, c)
        rows = pl.ds(c * tile, tile)
        base[rows, :] = r[:, :tile] - b2 + bias
        fw1[rows, :] = r[:, tile : 2 * tile]

    gather(fld1, sems1, True)
    for c in order:
        rows = pl.ds(c * tile, tile)
        fld2[me, c] = (fw1[rows, :] + 2.0 * (acc[rows, :] * inv_ref[rows, :])).astype(BF16)
        emit_own(fld2, sems2, c)
    gather(fld2, sems2, False)
    out_ref[...] = (base[...] + acc[...] * inv_ref[...]).astype(BF16)
    for kind in range(3):
        for c in range(rt):
            x_copy(kind, c).wait_send()
    drain(fld1, sems1)
    drain(fld2, sems2)


def fast(features, tile_values, tile_source, tile_target, tile_count, weights, bias_vector):
    tile = tile_values.shape[1]
    rows, cols = features.shape
    rt = rows // tile
    blocks = lax.axis_size("blk")
    levels = blocks // 2
    a, inv = build(tile_values, tile_source, tile_target, tile_count, rt, blocks)
    vmem = pl.BlockSpec(memory_space=pltpu.VMEM)
    hbm = pl.BlockSpec(memory_space=pltpu.HBM)
    dma = pltpu.SemaphoreType.DMA
    gather_sems = [
        dma((2, levels - 1, rt + 1)), dma((2, levels - 1, rt + 1)),
        dma((2 * levels - 1, rt)), dma((2 * levels - 1, rt)),
    ]
    return pl.pallas_call(
        functools.partial(main_kernel, levels),
        out_shape=jax.ShapeDtypeStruct((rows, cols), BF16),
        in_specs=[vmem, hbm, vmem, vmem, hbm],
        out_specs=vmem,
        scratch_shapes=[
            pltpu.VMEM((3, rt, tile, tile), BF16),
            pltpu.VMEM((blocks, rt, tile, tile), BF16),
            pltpu.VMEM((blocks, rt, tile, tile), BF16),
            pltpu.VMEM((blocks, rows, rows), BF16),
            pltpu.VMEM((4, tile, 3 * tile), BF16),
            pltpu.VMEM((rows, tile), F32),
            pltpu.VMEM((rows, tile), F32),
            pltpu.VMEM((rows, tile), F32),
            dma((blocks,)),
            dma((4, 3)),
            dma((3, rt)),
            dma((3, rt)),
        ] + gather_sems + gather_sems,
        compiler_params=pltpu.CompilerParams(collective_id=0, has_side_effects=True, vmem_limit_bytes=32 << 20),
        name="propagate",
    )(features.reshape(rt, tile, cols), weights, bias_vector.reshape(1, -1), inv, a)


def per_device(features, tile_values, tile_source, tile_target, tile_count, weights, bias_vector):
    tile_size = tile_values.shape[1]
    slot_total = tile_values.shape[0]
    channels = features.shape[1]
    row_tiles = features.shape[0] // tile_size
    block_rows = row_tiles * tile_size
    block_count = lax.axis_size("blk")
    slot_cap = max(2, (2 * slot_total + block_count - 1) // block_count)
    usable = jnp.arange(slot_total, dtype=jnp.int32) < tile_count[0]
    squares = jnp.einsum(
        "tij,tij->ti", tile_values, tile_values, preferred_element_type=jnp.float32
    )
    squares = jnp.where(usable[:, None], squares, 0.0)
    onehot = (
        (tile_target[:, None] == jnp.arange(row_tiles, dtype=jnp.int32)[None, :]) & usable[:, None]
    ).astype(jnp.float32)
    row_norm = jnp.dot(onehot.T, squares, precision=lax.Precision.HIGHEST)
    inverse = lax.rsqrt(1.0 + row_norm).reshape(-1)
    zero_sum = jnp.zeros((row_tiles, tile_size, channels), jnp.float32)

    def cycle_prop(signal):
        segment = lax.all_gather(signal, "blk", axis=0, tiled=True)
        offset = jnp.int32(0)
        count_rows = segment.shape[0]
        window = min(slot_total, slot_cap * (count_rows // block_rows + 2))
        low_row = tile_source * tile_size
        first_slot = jnp.sum(usable & (low_row + tile_size <= offset))
        end_slot = jnp.sum(usable & (low_row < offset + count_rows))
        start_slot = jnp.minimum(first_slot, slot_total - window)
        slot_ids = start_slot + jnp.arange(window, dtype=jnp.int32)
        in_range = (slot_ids >= first_slot) & (slot_ids < end_slot)
        row_ids = tile_source[:, None] * tile_size + jnp.arange(tile_size, dtype=jnp.int32)[None, :]
        inside = (row_ids >= 0) & (row_ids < count_rows) & in_range[:, None]
        picked = jnp.take(segment, jnp.clip(row_ids, 0, count_rows - 1).reshape(-1), axis=0)
        picked = picked.reshape(window, tile_size, channels)
        picked = jnp.where(inside[:, :, None], picked, jnp.zeros((), segment.dtype))
        product = jnp.einsum(
            "gij,gjc->gic", tile_values, picked, preferred_element_type=jnp.float32
        )
        product = jnp.where(in_range[:, None, None], product, 0.0)
        summed = zero_sum.at[tile_target].add(product)
        return summed.reshape(-1, channels) * inverse[:, None]

    col_start = lax.axis_index("ch") * channels
    bias_part = lax.dynamic_slice_in_dim(bias_vector, col_start, channels, 0)
    w_cols = lax.dynamic_slice_in_dim(weights, col_start, channels, 2)

    def mix_term(order_term, order_index, running):
        w_slice = w_cols[order_index]
        return running + jnp.dot(
            lax.all_gather(order_term, "ch", axis=1, tiled=True),
            w_slice,
            preferred_element_type=jnp.float32,
        )

    result = mix_term(features, 0, jnp.zeros((features.shape[0], channels), jnp.float32))
    first_order = cycle_prop(features).astype(jnp.bfloat16)
    result = mix_term(first_order, 1, result)
    second_order = (2.0 * cycle_prop(first_order) - features.astype(jnp.float32)).astype(
        jnp.bfloat16
    )
    result = mix_term(second_order, 2, result)
    return (result + bias_part[None, :]).astype(jnp.bfloat16)


def solution(mesh):
    dense = mesh.shape["blk"] == 8 and mesh.shape["ch"] == 4
    return jax.shard_map(
        fast if dense else per_device,
        mesh=mesh,
        in_specs=(P("blk", "ch"), P("blk", None, None), P("blk"), P("blk"), P("blk"), P(), P()),
        out_specs=P("blk", "ch"),
        check_vma=False,
    )
```
